32 devices in a mesh: pipe: 2 (over core), seq: 4 (over z), dp: 4 (over y, x).
Axes of the slice: x: 2, y: 2, z: 4, core: 2. Of those that a mesh axis runs over, the one named last changes fastest.
Arguments:
- inputs: bfloat16 [2, 4, 1024, 2048], P(None, 'dp', 'seq'), may hold values from -6 to 6
- cotangent: bfloat16 [2, 4, 1024, 2048], P(None, 'dp', 'seq'), may hold values from -6 to 6
- lengths: int32 [2, 4], replicated, may hold values from 256 to 1024, as said below
- norm_gain: float32 [2, 2048], P('pipe'), may hold values from 0.5 to 1.5
- w_query: float32 [2, 2048, 2048], P('pipe', None, 'seq'), may hold values from -0.125 to 0.125
- w_forget: float32 [2, 2048, 2048], P('pipe', None, 'seq'), may hold values from -0.125 to 0.125
- w_input: float32 [2, 2048, 2048], P('pipe', None, 'seq'), may hold values from -0.125 to 0.125
- lower_bound: float32 [2, 2048], P('pipe', 'seq'), may hold values from 0.4 to 0.9998
- out_gain: float32 [2, 2048], P('pipe', 'seq'), may hold values from 0.5 to 1.5
- w_output: float32 [2, 2048, 2048], P('pipe', 'seq'), may hold values from -0.125 to 0.125
- ffn_gain: float32 [2, 2048], P('pipe'), may hold values from 0.5 to 1.5
- w_gate: float32 [2, 2048, 5632], P('pipe', None, 'seq'), may hold values from -0.125 to 0.125
- w_up: float32 [2, 2048, 5632], P('pipe', None, 'seq'), may hold values from -0.125 to 0.125
- w_down: float32 [2, 5632, 2048], P('pipe', 'seq'), may hold values from -0.078125 to 0.078125
Outputs:
- section_outputs: bfloat16 [2, 2, 4, 1024, 2048], P('pipe', None, 'dp', 'seq')
- input_grads: float32 [2, 2, 4, 1024, 2048], P('pipe', None, 'dp', 'seq')
- grad_norm_gain: float32 [2, 2048], P('pipe')
- grad_query: float32 [2, 2048, 2048], P('pipe', None, 'seq')
- grad_forget: float32 [2, 2048, 2048], P('pipe', None, 'seq')
- grad_input: float32 [2, 2048, 2048], P('pipe', None, 'seq')
- grad_lower_bound: float32 [2, 2048], P('pipe', 'seq')
- grad_out_gain: float32 [2, 2048], P('pipe', 'seq')
- grad_output: float32 [2, 2048, 2048], P('pipe', 'seq')
- grad_ffn_gain: float32 [2, 2048], P('pipe')
- grad_gate: float32 [2, 2048, 5632], P('pipe', None, 'seq')
- grad_up: float32 [2, 2048, 5632], P('pipe', None, 'seq')
- grad_down: float32 [2, 5632, 2048], P('pipe', 'seq')
The draws below stay inside these ranges and needn't reach their ends.
Inputs may be any that keep to these rules, and one draw needn't show every extreme that they name: `lengths`: each micro-batch holds one sequence in each row, its valid tokens at the start of the row; some row is full (1024) and some has exactly 256.
All inputs are finite; a program needn't handle non-finite values.
Results may differ from the reference program's by a relative error of at most 0.035.
Values may be sent and summed in bfloat16 or wider, within the bound.
A program may use at most 576 MiB of HBM per device.

```python
import math
import jax
import jax.numpy as jnp
from jax import lax

D = 2048
HEADS = 16
FF = 5632
MB = 2
SLOTS = 1024
SEQS = 4
SECTIONS = 2
SPAN = 64
BLOCK = 512


def draw_lengths(key, part):
    row_count = MB * SEQS
    key_drawn, key_long, key_short = jax.random.split(jax.random.fold_in(key, 11), 3)
    drawn_lengths = jax.random.randint(key_drawn, (row_count,), SLOTS // 4, SLOTS + 1)
    longest = jax.random.randint(key_long, (), 0, row_count)
    shortest = (longest + 1 + jax.random.randint(key_short, (), 0, row_count - 1)) % row_count
    drawn_lengths = drawn_lengths.at[longest].set(SLOTS).at[shortest].set(SLOTS // 4)
    return drawn_lengths.reshape(MB, SEQS).astype(jnp.int32)


def draw_lower_bound(key, part):
    spread = jax.random.uniform(jax.random.fold_in(key, 23), (SECTIONS, D), jnp.float32, math.log(0.0002), math.log(0.6))
    return (1.0 - jnp.exp(spread)).astype(jnp.float32)


def levels(rng, dims, cuts, smallest, largest):
    level, own = 1.0, jax.random.fold_in(rng, 6)
    for dim, blocks in cuts:
        heights = jnp.exp(jax.random.uniform(jax.random.fold_in(own, dim), (blocks,), jnp.float32, smallest / len(cuts), largest / len(cuts)))
        level = level * jnp.repeat(heights, dims[dim] // blocks).reshape([-1 if axis == dim else 1 for axis in range(len(dims))])
    return level


def normal_values(key, dims, scale, limit, cuts=(), held_as=jnp.bfloat16):
    level = levels(key, dims, cuts, -0.22, 0.18) if cuts else 1.0
    drawn = jax.random.normal(key, dims, jnp.float32) * scale * level
    return jnp.minimum(jnp.maximum(drawn, -limit), limit).astype(held_as)


def setup_inputs(seed: int = 0) -> dict:
    key_of = jax.random.split(jax.random.key(seed), 15)
    inputs = normal_values(key_of[0], (MB, SEQS, SLOTS, D), 1.0, 6.0, ((1, 4), (2, 4)))
    cotangent = normal_values(key_of[1], (MB, SEQS, SLOTS, D), 1.0, 6.0, ((1, 4), (2, 4)))
    lengths = draw_lengths(jax.random.fold_in(key_of[14], 71), 0)
    norm_gain = jnp.clip(1.0 + 0.1 * jax.random.normal(key_of[3], (SECTIONS, D), jnp.float32), 0.5, 1.5)
    w_query = normal_values(key_of[4], (SECTIONS, D, D), D ** -0.5, 0.125, ((0, 2), (2, 4)), jnp.float32)
    w_forget = normal_values(key_of[5], (SECTIONS, D, D), D ** -0.5, 0.125, ((0, 2), (2, 4)), jnp.float32)
    w_input = normal_values(key_of[6], (SECTIONS, D, D), D ** -0.5, 0.125, ((0, 2), (2, 4)), jnp.float32)
    lower_bound = draw_lower_bound(jax.random.fold_in(key_of[14], 71), 0)
    out_gain = jnp.clip(1.0 + 0.1 * jax.random.normal(key_of[8], (SECTIONS, D), jnp.float32), 0.5, 1.5)
    w_output = normal_values(key_of[9], (SECTIONS, D, D), D ** -0.5, 0.125, ((0, 2), (1, 4)), jnp.float32)
    ffn_gain = jnp.clip(1.0 + 0.1 * jax.random.normal(key_of[10], (SECTIONS, D), jnp.float32), 0.5, 1.5)
    w_gate = normal_values(key_of[11], (SECTIONS, D, FF), D ** -0.5, 0.125, ((0, 2), (2, 4)), jnp.float32)
    w_up = normal_values(key_of[12], (SECTIONS, D, FF), D ** -0.5, 0.125, ((0, 2), (2, 4)), jnp.float32)
    w_down = normal_values(key_of[13], (SECTIONS, FF, D), FF ** -0.5, 0.078125, ((0, 2), (1, 4)), jnp.float32)
    return {"inputs": inputs, "cotangent": cotangent, "lengths": lengths, "norm_gain": norm_gain, "w_query": w_query, "w_forget": w_forget, "w_input": w_input, "lower_bound": lower_bound, "out_gain": out_gain, "w_output": w_output, "ffn_gain": ffn_gain, "w_gate": w_gate, "w_up": w_up, "w_down": w_down}


EPSILON = 1e-06

@jax.custom_vjp
def low(v):
    return lax.optimization_barrier(v.astype(jnp.bfloat16)).astype(jnp.float32)

@jax.custom_vjp
def low_back(v):
    return v

def low_keep(v):
    return (low(v), None)

def low_pass(kept, grad):
    return (grad,)

def back_keep(v):
    return (v, None)

def back_low(kept, grad):
    return (low(grad),)
low.defvjp(low_keep, low_pass)
low_back.defvjp(back_keep, back_low)

def rms_norm(values_in, gain):
    return values_in * lax.rsqrt(lax.optimization_barrier(jnp.mean(values_in * values_in, axis=-1, keepdims=True)) + EPSILON) * gain

def matmul(left, right):
    return jnp.dot(left, right, precision=lax.Precision.HIGHEST)

def gate_terms(forget_raw, bound):
    forget_log = jnp.log(bound + (1.0 - bound) * jax.nn.sigmoid(forget_raw))
    keys_in = (1.0 - bound) * jax.nn.sigmoid(-forget_raw)
    return (forget_log, keys_in)

def intra_part(parts):
    query_blocks, key_blocks, value_blocks, cumul = parts
    differ = cumul[:, :, None] - cumul[:, None, :]
    lower = (jnp.arange(SPAN)[:, None] >= jnp.arange(SPAN)[None, :]).astype(jnp.float32)
    weight = jnp.exp(jnp.minimum(differ, 0.0)) * lower[None, :, :, None, None]
    scores = lax.optimization_barrier(jnp.sum(weight * query_blocks[:, :, None] * key_blocks[:, None, :], axis=-1))
    return jnp.einsum('ntsh,nshe->nthe', scores, value_blocks, precision=lax.Precision.HIGHEST)

def recurrence(queries, forget_log, keys_in, values_in):
    length, heads_count, head_dim = queries.shape
    spans = length // SPAN
    shape_four = (spans, SPAN, heads_count, head_dim)
    query_blocks = queries.reshape(shape_four)
    key_blocks = keys_in.reshape(shape_four)
    value_blocks = values_in.reshape(shape_four)
    cumul = jnp.cumsum(forget_log.reshape(shape_four), axis=1)
    ending = cumul[:, -1]
    weighted_keys = key_blocks * jnp.exp(ending[:, None] - cumul)
    updates = jnp.einsum('nchd,nche->nhde', weighted_keys, value_blocks, precision=lax.Precision.HIGHEST)
    decays = jnp.exp(ending)

    def advance(state, pair):
        update, decay = pair
        return (decay[..., None] * state + update, state)
    start_state = jnp.zeros((heads_count, head_dim, head_dim), jnp.float32)
    _, before = lax.scan(advance, start_state, (updates, decays))
    carried = jnp.einsum('nchd,nhde->nche', query_blocks * jnp.exp(cumul), before, precision=lax.Precision.HIGHEST)
    per_group = BLOCK // SPAN
    groups = spans // per_group

    def regroup(array_in):
        return array_in.reshape((groups, per_group) + array_in.shape[1:])
    within = lax.map(jax.checkpoint(intra_part), (regroup(query_blocks), regroup(key_blocks), regroup(value_blocks), regroup(cumul)))
    result = carried + within.reshape(shape_four)
    return result.reshape(length, heads_count, head_dim)

def block(inputs_row, mask_row, params):
    norm_gain, w_query, w_forget, w_input, lower_bound, out_gain, w_output, ffn_gain, w_gate, w_up, w_down = params
    length = inputs_row.shape[0]
    head_dim = D // HEADS
    normed = low(rms_norm(inputs_row, norm_gain))
    queries = low_back(matmul(normed, w_query))
    forget_raw = low_back(matmul(normed, w_forget))
    values_in = low_back(matmul(normed, w_input))
    forget_log, keys_in = gate_terms(forget_raw, lower_bound)
    shape_three = (length, HEADS, head_dim)
    mixed = recurrence(queries.reshape(shape_three), forget_log.reshape(shape_three), keys_in.reshape(shape_three), values_in.reshape(shape_three)).reshape(length, D)
    branch = low_back(matmul(low(rms_norm(mixed, out_gain)), w_output))
    middle = inputs_row + branch
    normed_two = low(rms_norm(middle, ffn_gain))
    gate_act = low_back(matmul(normed_two, w_gate))
    up_act = low_back(matmul(normed_two, w_up))
    hidden = low(jax.nn.silu(gate_act) * up_act)
    ffn_branch = low_back(matmul(hidden, w_down))
    return mask_row[:, None] * (middle + ffn_branch)

def run_section(section_in, cots, token_mask, params):

    def one_row(accum, row):
        inputs_row, cot_row, mask_row = row

        def forward_fn(param_tuple, values_row):
            return block(values_row, mask_row, param_tuple)
        outputs, pull = jax.vjp(forward_fn, params, inputs_row)
        grad_params, grad_inputs = pull(cot_row)
        accum = jax.tree.map(lambda left, right: left + right, accum, grad_params)
        return (accum, (outputs, grad_inputs))
    empty = jax.tree.map(jnp.zeros_like, params)
    return lax.scan(one_row, empty, (section_in, cots, token_mask))

def reference(inputs, cotangent, lengths, norm_gain, w_query, w_forget, w_input, lower_bound, out_gain, w_output, ffn_gain, w_gate, w_up, w_down):
    row_count = MB * SEQS
    positions = jnp.arange(SLOTS, dtype=jnp.int32)
    token_mask = (positions[None, None, :] < lengths[:, :, None]).astype(jnp.float32).reshape(row_count, SLOTS)
    section_in = inputs.astype(jnp.float32).reshape(row_count, SLOTS, D)
    cots = cotangent.astype(jnp.float32).reshape(row_count, SLOTS, D)
    weights = (norm_gain, w_query, w_forget, w_input, lower_bound, out_gain, w_output, ffn_gain, w_gate, w_up, w_down)
    section_zero = tuple((array_in[0].astype(jnp.float32) for array_in in weights))
    section_one = tuple((array_in[1].astype(jnp.float32) for array_in in weights))
    first_out = lax.map(lambda pair: block(pair[0], pair[1], section_zero), (section_in, token_mask))
    grads_one, (second_out, grad_one_in) = run_section(low(first_out), cots, token_mask, section_one)
    grads_zero, (_, grad_zero_in) = run_section(section_in, low(grad_one_in), token_mask, section_zero)
    shape_five = (MB, SEQS, SLOTS, D)
    section_outputs = jnp.stack([first_out.reshape(shape_five), second_out.reshape(shape_five)]).astype(jnp.bfloat16)
    input_grads = jnp.stack([grad_zero_in.reshape(shape_five), grad_one_in.reshape(shape_five)])
    grads = [jnp.stack([zero_grad, one_grad]) for zero_grad, one_grad in zip(grads_zero, grads_one)]
    return (section_outputs, input_grads, grads[0], grads[1], grads[2], grads[3], grads[4], grads[5], grads[6], grads[7], grads[8], grads[9], grads[10])
```

```python
import jax
import jax.numpy as jnp
from jax import lax
from jax.experimental import pallas as pl
from jax.experimental.pallas import tpu as pltpu
from jax.sharding import PartitionSpec as P

EPSILON = 1e-06
SPAN = 128
HEAD = 128
HIGH = lax.Precision.HIGHEST


def mm(a, b, ca, cb):
    return lax.dot_general(
        a.astype(jnp.bfloat16),
        b.astype(jnp.bfloat16),
        (((ca,), (cb,)), ((), ())),
        preferred_element_type=jnp.float32,
    )


def gates(raw, lb):
    small = jnp.exp(-jnp.abs(raw))
    inv = 1.0 / (1.0 + small)
    sig = jnp.where(raw >= 0, inv, small * inv)
    nsig = jnp.where(raw >= 0, small * inv, inv)
    forget = lb + (1.0 - lb) * sig
    return sig, nsig, forget


def lower_mask():
    rows = lax.broadcasted_iota(jnp.int32, (SPAN, SPAN), 0)
    cols = lax.broadcasted_iota(jnp.int32, (SPAN, SPAN), 1)
    return rows >= cols


def rec_fwd_kernel(proj_ref, lb_ref, gain_ref, mg_ref, sq_ref, st_ref, state):
    width = lb_ref.shape[1]

    @pl.when(pl.program_id(0) == 0)
    def _():
        state[...] = jnp.zeros_like(state)

    lb = lb_ref[...]
    causal = lower_mask()
    _, nsig, forget = gates(proj_ref[:, width : 2 * width], lb)
    keys = (1.0 - lb) * nsig
    cumul = lax.dot_general(
        causal.astype(jnp.float32),
        jnp.log(forget),
        (((1,), (0,)), ((), ())),
        precision=HIGH,
        preferred_element_type=jnp.float32,
    )
    middle = cumul[SPAN // 2 - 1 : SPAN // 2]
    ending = cumul[SPAN - 1 : SPAN]
    to_mid = jnp.exp(middle)
    to_end = jnp.exp(ending - middle)
    decay = jnp.exp(ending)
    q_mid = proj_ref[:, :width] * jnp.exp(cumul - middle)
    k_mid = keys * jnp.exp(middle - cumul)
    q_start = q_mid * to_mid
    k_end = k_mid * to_end
    total = jnp.zeros((8, SPAN), jnp.float32)
    ones = jnp.ones((8, HEAD), jnp.float32)
    for head in range(width // HEAD):
        cut = slice(head * HEAD, (head + 1) * HEAD)
        vals = proj_ref[:, 2 * width + head * HEAD : 2 * width + (head + 1) * HEAD]
        before = state[head]
        st_ref[0, head] = before
        scores = jnp.where(causal, mm(q_mid[:, cut], k_mid[:, cut], 1, 1), 0.0)
        mixed = mm(scores, vals, 1, 0) + mm(q_start[:, cut], before, 1, 1)
        state[head] = decay[:, cut] * before + mm(vals, k_end[:, cut], 0, 0)
        total += lax.dot_general(
            ones,
            mixed * mixed,
            (((1,), (1,)), ((), ())),
            precision=HIGH,
            preferred_element_type=jnp.float32,
        )
        mg_ref[:, cut] = (mixed * gain_ref[:, cut]).astype(jnp.bfloat16)
    sq_ref[...] = total


def rec_bwd_kernel(proj_ref, st_ref, dm_ref, lb_ref, dproj_ref, glb_ref, dstate):
    width = lb_ref.shape[1]

    @pl.when(pl.program_id(0) == 0)
    def _():
        dstate[...] = jnp.zeros_like(dstate)
        glb_ref[...] = jnp.zeros_like(glb_ref)

    lb = lb_ref[...]
    causal = lower_mask()
    lower = causal.astype(jnp.float32)
    sig, nsig, forget = gates(proj_ref[:, width : 2 * width], lb)
    keys = (1.0 - lb) * nsig
    cumul = lax.dot_general(
        lower,
        jnp.log(forget),
        (((1,), (0,)), ((), ())),
        precision=HIGH,
        preferred_element_type=jnp.float32,
    )
    middle = cumul[SPAN // 2 - 1 : SPAN // 2]
    ending = cumul[SPAN - 1 : SPAN]
    to_mid = jnp.exp(middle)
    to_end = jnp.exp(ending - middle)
    decay = jnp.exp(ending)
    eq = jnp.exp(cumul - middle)
    ek = jnp.exp(middle - cumul)
    q_mid = (proj_ref[:, :width] * eq).astype(jnp.bfloat16)
    k_mid = (keys * ek).astype(jnp.bfloat16)
    for head in range(width // HEAD):
        cut = slice(head * HEAD, (head + 1) * HEAD)
        vals = proj_ref[:, 2 * width + head * HEAD : 2 * width + (head + 1) * HEAD].astype(
            jnp.bfloat16
        )
        qm, km = q_mid[:, cut], k_mid[:, cut]
        qf, kf = qm.astype(jnp.float32), km.astype(jnp.float32)
        qs = qf * to_mid[:, cut]
        ke = kf * to_end[:, cut]
        before = st_ref[0, head]
        after = dstate[head]
        dmix = dm_ref[:, cut]
        scores = jnp.where(causal, mm(qm, km, 1, 1), 0.0)
        dscores = jnp.where(causal, mm(dmix, vals, 1, 1), 0.0).astype(jnp.bfloat16)
        dq_in = mm(dscores, km, 1, 0)
        dk_in = mm(dscores, qm, 0, 0)
        dq_out = mm(dmix, before, 1, 0)
        dk_out = mm(vals, after, 1, 0)
        dvals = mm(scores, dmix, 0, 0) + mm(ke, after, 1, 1)
        flow = ke * dk_out
        change = qf * dq_in - kf * dk_in + qs * dq_out - flow
        edge = jnp.sum(flow, axis=0, keepdims=True) + decay[:, cut] * jnp.sum(
            before * after, axis=0, keepdims=True
        )
        dlog = (
            lax.dot_general(
                lower,
                change,
                (((0,), (0,)), ((), ())),
                precision=HIGH,
                preferred_element_type=jnp.float32,
            )
            + edge
        )
        dqueries = eq[:, cut] * (dq_in + to_mid[:, cut] * dq_out)
        dkeys = ek[:, cut] * (dk_in + to_end[:, cut] * dk_out)
        lbh, sg, ns = lb[:, cut], sig[:, cut], nsig[:, cut]
        ratio = dlog / forget[:, cut] - dkeys
        draw = ratio * ((1.0 - lbh) * sg * ns)
        glb_ref[:, cut] += jnp.broadcast_to(
            jnp.sum(ratio * ns, axis=0, keepdims=True), (8, HEAD)
        )
        dstate[head] = decay[:, cut] * after + mm(dmix, qs, 0, 0)
        dproj_ref[:, cut] = dqueries.astype(jnp.bfloat16)
        dproj_ref[:, width + head * HEAD : width + (head + 1) * HEAD] = draw.astype(jnp.bfloat16)
        dproj_ref[:, 2 * width + head * HEAD : 2 * width + (head + 1) * HEAD] = dvals.astype(
            jnp.bfloat16
        )


def rec_fwd(proj, lb, gain):
    length, width = proj.shape[0], lb.shape[0]
    spans, heads = length // SPAN, width // HEAD
    return pl.pallas_call(
        rec_fwd_kernel,
        grid=(spans,),
        in_specs=[
            pl.BlockSpec((SPAN, 3 * width), lambda i: (i, 0)),
            pl.BlockSpec((1, width), lambda i: (0, 0)),
            pl.BlockSpec((1, width), lambda i: (0, 0)),
        ],
        out_specs=[
            pl.BlockSpec((SPAN, width), lambda i: (i, 0)),
            pl.BlockSpec((8, SPAN), lambda i: (0, i)),
            pl.BlockSpec((1, heads, HEAD, HEAD), lambda i: (i, 0, 0, 0)),
        ],
        out_shape=[
            jax.ShapeDtypeStruct((length, width), jnp.bfloat16),
            jax.ShapeDtypeStruct((8, length), jnp.float32),
            jax.ShapeDtypeStruct((spans, heads, HEAD, HEAD), jnp.float32),
        ],
        scratch_shapes=[pltpu.VMEM((heads, HEAD, HEAD), jnp.float32)],
        cost_estimate=pl.CostEstimate(
            flops=8 * length * SPAN * width,
            bytes_accessed=20 * length * width,
            transcendentals=8 * length * width,
        ),
        name="rec_fwd",
    )(proj, lb[None], gain[None])


def rec_bwd(proj, states, dmix, lb):
    length, width = proj.shape[0], lb.shape[0]
    spans, heads = length // SPAN, width // HEAD
    dproj, glb = pl.pallas_call(
        rec_bwd_kernel,
        grid=(spans,),
        in_specs=[
            pl.BlockSpec((SPAN, 3 * width), lambda i: (spans - 1 - i, 0)),
            pl.BlockSpec((1, heads, HEAD, HEAD), lambda i: (spans - 1 - i, 0, 0, 0)),
            pl.BlockSpec((SPAN, width), lambda i: (spans - 1 - i, 0)),
            pl.BlockSpec((1, width), lambda i: (0, 0)),
        ],
        out_specs=[
            pl.BlockSpec((SPAN, 3 * width), lambda i: (spans - 1 - i, 0)),
            pl.BlockSpec((8, width), lambda i: (0, 0)),
        ],
        out_shape=[
            jax.ShapeDtypeStruct((length, 3 * width), jnp.bfloat16),
            jax.ShapeDtypeStruct((8, width), jnp.float32),
        ],
        scratch_shapes=[pltpu.VMEM((heads, HEAD, HEAD), jnp.float32)],
        cost_estimate=pl.CostEstimate(
            flops=20 * length * SPAN * width,
            bytes_accessed=30 * length * width,
            transcendentals=8 * length * width,
        ),
        name="rec_bwd",
    )(proj, states, dmix, lb[None])
    return dproj, glb[0]


def other_core(array):
    return lax.ppermute(array, "pipe", [(0, 1), (1, 0)])


def small_sum(array, axis):
    size = lax.axis_size(axis)
    if size > 4:
        return lax.psum(array, axis)
    total = array
    for step in range(1, size):
        total = total + lax.ppermute(array, axis, [(i, (i + step) % size) for i in range(size)])
    return total


def pick(first, zero, one):
    return jnp.where(first, zero, one)


def inverse_rms(values_in):
    return lax.rsqrt(jnp.mean(values_in * values_in, axis=-1, keepdims=True) + EPSILON)


def norm_backward(values_in, gain, grad):
    inv = inverse_rms(values_in)
    unit = values_in * inv
    grad_gain = jnp.sum(grad * unit, axis=0)
    scaled = grad * gain
    return inv * (scaled - unit * jnp.mean(scaled * unit, axis=-1, keepdims=True)), grad_gain


def dot(left, right, left_dim, right_dim, kind=jnp.float32):
    return lax.dot_general(
        left, right, (((left_dim,), (right_dim,)), ((), ())), preferred_element_type=jnp.float32
    ).astype(kind)


def gather_rows(array):
    return lax.all_gather(array, "seq", axis=0, tiled=True)


def scatter_rows(array):
    return lax.psum_scatter(array, "seq", scatter_dimension=0, tiled=True).astype(jnp.float32)


def pair_moves(step):
    count = lax.axis_size("dp")
    return [(i, i ^ step) for i in range(count)]


def start_sum(grad):
    core = lax.axis_index("pipe")
    row = lax.axis_index("dp")
    count = lax.axis_size("dp")
    rows, columns = grad.shape
    halves = grad.reshape(2, rows // 2, columns)
    keep = lax.dynamic_index_in_dim(halves, core, 0, keepdims=False)
    send = lax.dynamic_index_in_dim(halves, 1 - core, 0, keepdims=False)
    half = (
        keep.astype(jnp.float32) + other_core(send).astype(jnp.float32)
    ).astype(jnp.bfloat16)
    parts = half.reshape(count, rows // (2 * count), columns)
    total = lax.dynamic_index_in_dim(parts, row, 0, keepdims=False).astype(jnp.float32)
    for step in range(1, count):
        away = lax.dynamic_index_in_dim(parts, row ^ step, 0, keepdims=False)
        total = total + lax.ppermute(away, "dp", pair_moves(step)).astype(jnp.float32)
    return total.astype(jnp.bfloat16)


def finish_sum(zero, one):
    core = lax.axis_index("pipe")
    row = lax.axis_index("dp")
    count = lax.axis_size("dp")
    first = core == 0
    own = pick(first, zero, one)
    swapped = other_core(pick(first, one, zero))
    rows, columns = own.shape
    whole = jnp.zeros((2, count, rows, columns), jnp.float32)

    def put(whole, piece, half, place):
        return lax.dynamic_update_slice(
            whole, piece.astype(jnp.float32)[None, None], (half, place, 0, 0)
        )

    for half, piece in ((core, own), (1 - core, swapped)):
        whole = put(whole, piece, half, row)
        for step in range(1, count):
            whole = put(whole, lax.ppermute(piece, "dp", pair_moves(step)), half, row ^ step)
    return whole.reshape(2 * count * rows, columns)


def body(
    inputs,
    cotangent,
    lengths,
    norm_gain,
    w_query,
    w_forget,
    w_input,
    lower_bound,
    out_gain,
    w_output,
    ffn_gain,
    w_gate,
    w_up,
    w_down,
):
    local_rows, width = inputs.shape[2], inputs.shape[3]
    local_width = w_query.shape[2]
    hidden_here = w_gate.shape[2]
    core = lax.axis_index("pipe")
    row = lax.axis_index("dp")
    place = lax.axis_index("seq")
    first = core == 0
    bf16 = jnp.bfloat16

    def both(array):
        return lax.all_gather(array, "pipe", axis=0, tiled=False)

    w_proj_both = both(jnp.concatenate([w_query[0], w_forget[0], w_input[0]], axis=1).astype(bf16))
    w_out_both = both(w_output[0].astype(bf16))
    w_pair_both = both(jnp.concatenate([w_gate[0], w_up[0]], axis=1).astype(bf16))
    w_down_both = both(w_down[0].astype(bf16))
    gains = both(jnp.stack([norm_gain[0], ffn_gain[0]]))
    bounds = both(jnp.stack([lower_bound[0], out_gain[0]]))

    own_length = lax.dynamic_slice(lengths, (core, row), (1, 1))[0, 0]
    positions = place * local_rows + jnp.arange(local_rows, dtype=jnp.int32)
    mask = (positions < own_length).astype(jnp.float32)[:, None]
    block_in = lax.dynamic_index_in_dim(inputs, core, 0, keepdims=False)[0]
    source_grad = lax.dynamic_index_in_dim(cotangent, core, 0, keepdims=False)[0]

    saved = []
    outs = []
    for section in range(2):
        residual = block_in.astype(jnp.float32)
        normed = (residual * inverse_rms(residual) * gains[section, 0]).astype(bf16)
        normed_all = gather_rows(normed)
        projected = dot(normed_all, w_proj_both[section], 1, 0)
        head_gain = bounds[section, 1]
        mixed_gain, squares, states = rec_fwd(projected, bounds[section, 0], head_gain)
        squares = small_sum(squares[0], "seq")
        branch = scatter_rows(dot(mixed_gain, w_out_both[section], 1, 0, bf16))
        own_squares = lax.dynamic_slice(squares, (place * local_rows,), (local_rows,))
        inv_mix = lax.rsqrt(own_squares / width + EPSILON)[:, None]
        branch = branch * inv_mix
        middle = residual + branch
        normed_two = (middle * inverse_rms(middle) * gains[section, 1]).astype(bf16)
        normed_two_all = gather_rows(normed_two)
        paired = dot(normed_two_all, w_pair_both[section], 1, 0, bf16)
        gate_act = paired[:, :hidden_here].astype(jnp.float32)
        up_act = paired[:, hidden_here:].astype(jnp.float32)
        hidden = (jax.nn.silu(gate_act) * up_act).astype(bf16)
        ffn_branch = scatter_rows(dot(hidden, w_down_both[section], 1, 0, bf16))
        out_low = (mask * (middle + ffn_branch)).astype(bf16)
        outs.append(out_low)
        saved.append(
            (residual, normed_all, projected, mixed_gain, states, inv_mix, branch, middle)
            + (normed_two_all, paired, hidden)
        )
        block_in = out_low

    small = [None, None]
    shares = [None, None]
    grad_ins = [None, None]
    grad_out = source_grad.astype(jnp.float32)
    for section in (1, 0):
        residual, normed_all, projected, mixed_gain, states, inv_mix, branch, middle = saved[
            section
        ][:8]
        normed_two_all, paired, hidden = saved[section][8:]
        head_gain = bounds[section, 1]
        masked = mask * grad_out
        grad_branch_all = gather_rows(masked.astype(bf16))
        grad_hidden = dot(grad_branch_all, w_down_both[section], 1, 1)
        gate_act = paired[:, :hidden_here].astype(jnp.float32)
        up_act = paired[:, hidden_here:].astype(jnp.float32)
        sig = jax.nn.sigmoid(gate_act)
        grad_up = grad_hidden * gate_act * sig
        grad_gate = grad_hidden * up_act * sig * (1.0 + gate_act * (1.0 - sig))
        grad_pair = jnp.concatenate([grad_gate.astype(bf16), grad_up.astype(bf16)], axis=1)
        grad_normed_two = scatter_rows(dot(grad_pair, w_pair_both[section], 1, 1, bf16))
        grad_down = dot(hidden, grad_branch_all, 0, 0, bf16)
        grad_pair_weight = dot(normed_two_all, grad_pair, 0, 0, bf16)
        from_norm, grad_gain_two = norm_backward(middle, gains[section, 1], grad_normed_two)
        grad_middle = masked + from_norm
        inner = jnp.sum(grad_middle * branch, axis=1)
        factor = inv_mix[:, 0] * inv_mix[:, 0] * inner / width
        factor_all = small_sum(
            lax.dynamic_update_slice(
                jnp.zeros((local_rows * lax.axis_size("seq"),), jnp.float32),
                factor,
                (place * local_rows,),
            ),
            "seq",
        )
        grad_mix_all = gather_rows((grad_middle * inv_mix).astype(bf16))
        grad_head = dot(grad_mix_all, w_out_both[section], 1, 1)
        mixed = mixed_gain.astype(jnp.float32) / head_gain
        grad_head_gain = jnp.sum(grad_head * mixed, axis=0)
        grad_mixed = (grad_head * head_gain - mixed * factor_all[:, None]).astype(bf16)
        grad_proj, grad_bound = rec_bwd(projected, states, grad_mixed, bounds[section, 0])
        grad_normed = scatter_rows(dot(grad_proj, w_proj_both[section], 1, 1, bf16))
        grad_out_weight = dot(mixed_gain, grad_mix_all, 0, 0, bf16)
        grad_proj_weight = dot(normed_all, grad_proj, 0, 0, bf16)
        from_first, grad_gain_one = norm_backward(residual, gains[section, 0], grad_normed)
        grad_in = grad_middle + from_first
        grad_ins[section] = grad_in
        grad_out = grad_in.astype(bf16).astype(jnp.float32)
        spread = jnp.zeros((2, width), jnp.float32)
        spread = lax.dynamic_update_slice(
            spread, jnp.stack([grad_bound, grad_head_gain]), (0, place * local_width)
        )
        small[section] = jnp.concatenate([jnp.stack([grad_gain_one, grad_gain_two]), spread])
        shares[section] = [
            start_sum(part)
            for part in (grad_down, grad_pair_weight, grad_out_weight, grad_proj_weight)
        ]

    small_total = lax.psum(jnp.stack(small), ("pipe", "seq", "dp"))
    small_own = lax.dynamic_index_in_dim(small_total, core, 0, keepdims=False)
    local_small = lax.dynamic_slice(small_own, (2, place * local_width), (2, local_width))
    grad_down, grad_pair_weight, grad_out_weight, grad_proj_weight = [
        finish_sum(zero, one) for zero, one in zip(shares[0], shares[1])
    ]

    def exchange(zero, one):
        own = pick(first, zero, one)
        received = other_core(pick(first, one, zero))
        return jnp.stack([pick(first, own, received), pick(first, received, own)])[None, :, None]

    return (
        exchange(outs[0], outs[1]),
        exchange(grad_ins[0], grad_ins[1]),
        small_own[0][None],
        grad_proj_weight[:, :local_width][None],
        grad_proj_weight[:, local_width : 2 * local_width][None],
        grad_proj_weight[:, 2 * local_width :][None],
        local_small[0][None],
        local_small[1][None],
        grad_out_weight[None],
        small_own[1][None],
        grad_pair_weight[:, :hidden_here][None],
        grad_pair_weight[:, hidden_here:][None],
        grad_down[None],
    )


def solution(mesh):
    in_specs = (
        P(None, "dp", "seq", None),
        P(None, "dp", "seq", None),
        P(),
        P("pipe", None),
        P("pipe", None, "seq"),
        P("pipe", None, "seq"),
        P("pipe", None, "seq"),
        P("pipe", "seq"),
        P("pipe", "seq"),
        P("pipe", "seq", None),
        P("pipe", None),
        P("pipe", None, "seq"),
        P("pipe", None, "seq"),
        P("pipe", "seq", None),
    )
    out_specs = (
        P("pipe", None, "dp", "seq", None),
        P("pipe", None, "dp", "seq", None),
        P("pipe", None),
        P("pipe", None, "seq"),
        P("pipe", None, "seq"),
        P("pipe", None, "seq"),
        P("pipe", "seq"),
        P("pipe", "seq"),
        P("pipe", "seq", None),
        P("pipe", None),
        P("pipe", None, "seq"),
        P("pipe", None, "seq"),
        P("pipe", "seq", None),
    )
    return jax.shard_map(body, mesh=mesh, in_specs=in_specs, out_specs=out_specs, check_vma=False)
```

```python
import functools

import jax
import jax.numpy as jnp
from jax import lax
from jax.experimental import pallas as pl
from jax.experimental.pallas import tpu as pltpu
from jax.sharding import PartitionSpec as P

EPSILON = 1e-06
PIECES = 16
LAG = 2
SPAN = 128
HEAD = 128
HIGH = lax.Precision.HIGHEST


def mm(a, b, ca, cb):
    return lax.dot_general(
        a.astype(jnp.bfloat16),
        b.astype(jnp.bfloat16),
        (((ca,), (cb,)), ((), ())),
        preferred_element_type=jnp.float32,
    )


def gates(raw, lb):
    small = jnp.exp(-jnp.abs(raw))
    inv = 1.0 / (1.0 + small)
    sig = jnp.where(raw >= 0, inv, small * inv)
    nsig = jnp.where(raw >= 0, small * inv, inv)
    forget = lb + (1.0 - lb) * sig
    return sig, nsig, forget


def lower_mask():
    rows = lax.broadcasted_iota(jnp.int32, (SPAN, SPAN), 0)
    cols = lax.broadcasted_iota(jnp.int32, (SPAN, SPAN), 1)
    return rows >= cols


def rec_fwd_kernel(proj_ref, lb_ref, gain_ref, mg_ref, sq_ref, st_ref, state):
    width = lb_ref.shape[1]

    @pl.when(pl.program_id(0) == 0)
    def _():
        state[...] = jnp.zeros_like(state)

    lb = lb_ref[...]
    causal = lower_mask()
    _, nsig, forget = gates(proj_ref[:, width : 2 * width], lb)
    keys = (1.0 - lb) * nsig
    cumul = lax.dot_general(
        causal.astype(jnp.float32),
        jnp.log(forget),
        (((1,), (0,)), ((), ())),
        precision=HIGH,
        preferred_element_type=jnp.float32,
    )
    middle = cumul[SPAN // 2 - 1 : SPAN // 2]
    ending = cumul[SPAN - 1 : SPAN]
    to_mid = jnp.exp(middle)
    to_end = jnp.exp(ending - middle)
    decay = jnp.exp(ending)
    q_mid = proj_ref[:, :width] * jnp.exp(cumul - middle)
    k_mid = keys * jnp.exp(middle - cumul)
    q_start = q_mid * to_mid
    k_end = k_mid * to_end
    total = jnp.zeros((8, SPAN), jnp.float32)
    ones = jnp.ones((8, HEAD), jnp.float32)
    for head in range(width // HEAD):
        cut = slice(head * HEAD, (head + 1) * HEAD)
        vals = proj_ref[:, 2 * width + head * HEAD : 2 * width + (head + 1) * HEAD]
        before = state[head]
        st_ref[0, head] = before
        scores = jnp.where(causal, mm(q_mid[:, cut], k_mid[:, cut], 1, 1), 0.0)
        mixed = mm(scores, vals, 1, 0) + mm(q_start[:, cut], before, 1, 1)
        state[head] = decay[:, cut] * before + mm(vals, k_end[:, cut], 0, 0)
        total += lax.dot_general(
            ones,
            mixed * mixed,
            (((1,), (1,)), ((), ())),
            precision=HIGH,
            preferred_element_type=jnp.float32,
        )
        mg_ref[:, cut] = (mixed * gain_ref[:, cut]).astype(jnp.bfloat16)
    sq_ref[...] = total


def rec_bwd_kernel(proj_ref, st_ref, dm_ref, lb_ref, dproj_ref, glb_ref, dstate):
    width = lb_ref.shape[1]

    @pl.when(pl.program_id(0) == 0)
    def _():
        dstate[...] = jnp.zeros_like(dstate)
        glb_ref[...] = jnp.zeros_like(glb_ref)

    lb = lb_ref[...]
    causal = lower_mask()
    lower = causal.astype(jnp.float32)
    sig, nsig, forget = gates(proj_ref[:, width : 2 * width], lb)
    keys = (1.0 - lb) * nsig
    cumul = lax.dot_general(
        lower,
        jnp.log(forget),
        (((1,), (0,)), ((), ())),
        precision=HIGH,
        preferred_element_type=jnp.float32,
    )
    middle = cumul[SPAN // 2 - 1 : SPAN // 2]
    ending = cumul[SPAN - 1 : SPAN]
    to_mid = jnp.exp(middle)
    to_end = jnp.exp(ending - middle)
    decay = jnp.exp(ending)
    eq = jnp.exp(cumul - middle)
    ek = jnp.exp(middle - cumul)
    q_mid = (proj_ref[:, :width] * eq).astype(jnp.bfloat16)
    k_mid = (keys * ek).astype(jnp.bfloat16)
    for head in range(width // HEAD):
        cut = slice(head * HEAD, (head + 1) * HEAD)
        vals = proj_ref[:, 2 * width + head * HEAD : 2 * width + (head + 1) * HEAD].astype(
            jnp.bfloat16
        )
        qm, km = q_mid[:, cut], k_mid[:, cut]
        qf, kf = qm.astype(jnp.float32), km.astype(jnp.float32)
        qs = qf * to_mid[:, cut]
        ke = kf * to_end[:, cut]
        before = st_ref[0, head]
        after = dstate[head]
        dmix = dm_ref[:, cut]
        scores = jnp.where(causal, mm(qm, km, 1, 1), 0.0)
        dscores = jnp.where(causal, mm(dmix, vals, 1, 1), 0.0).astype(jnp.bfloat16)
        dq_in = mm(dscores, km, 1, 0)
        dk_in = mm(dscores, qm, 0, 0)
        dq_out = mm(dmix, before, 1, 0)
        dk_out = mm(vals, after, 1, 0)
        dvals = mm(scores, dmix, 0, 0) + mm(ke, after, 1, 1)
        flow = ke * dk_out
        change = qf * dq_in - kf * dk_in + qs * dq_out - flow
        edge = jnp.sum(flow, axis=0, keepdims=True) + decay[:, cut] * jnp.sum(
            before * after, axis=0, keepdims=True
        )
        dlog = (
            lax.dot_general(
                lower,
                change,
                (((0,), (0,)), ((), ())),
                precision=HIGH,
                preferred_element_type=jnp.float32,
            )
            + edge
        )
        dqueries = eq[:, cut] * (dq_in + to_mid[:, cut] * dq_out)
        dkeys = ek[:, cut] * (dk_in + to_end[:, cut] * dk_out)
        lbh, sg, ns = lb[:, cut], sig[:, cut], nsig[:, cut]
        ratio = dlog / forget[:, cut] - dkeys
        draw = ratio * ((1.0 - lbh) * sg * ns)
        glb_ref[:, cut] += jnp.broadcast_to(
            jnp.sum(ratio * ns, axis=0, keepdims=True), (8, HEAD)
        )
        dstate[head] = decay[:, cut] * after + mm(dmix, qs, 0, 0)
        dproj_ref[:, cut] = dqueries.astype(jnp.bfloat16)
        dproj_ref[:, width + head * HEAD : width + (head + 1) * HEAD] = draw.astype(jnp.bfloat16)
        dproj_ref[:, 2 * width + head * HEAD : 2 * width + (head + 1) * HEAD] = dvals.astype(
            jnp.bfloat16
        )


def rec_fwd(proj, lb, gain):
    length, width = proj.shape[0], lb.shape[0]
    spans, heads = length // SPAN, width // HEAD
    return pl.pallas_call(
        rec_fwd_kernel,
        grid=(spans,),
        in_specs=[
            pl.BlockSpec((SPAN, 3 * width), lambda i: (i, 0)),
            pl.BlockSpec((1, width), lambda i: (0, 0)),
            pl.BlockSpec((1, width), lambda i: (0, 0)),
        ],
        out_specs=[
            pl.BlockSpec((SPAN, width), lambda i: (i, 0)),
            pl.BlockSpec((8, SPAN), lambda i: (0, i)),
            pl.BlockSpec((1, heads, HEAD, HEAD), lambda i: (i, 0, 0, 0)),
        ],
        out_shape=[
            jax.ShapeDtypeStruct((length, width), jnp.bfloat16),
            jax.ShapeDtypeStruct((8, length), jnp.float32),
            jax.ShapeDtypeStruct((spans, heads, HEAD, HEAD), jnp.float32),
        ],
        scratch_shapes=[pltpu.VMEM((heads, HEAD, HEAD), jnp.float32)],
        cost_estimate=pl.CostEstimate(
            flops=8 * length * SPAN * width,
            bytes_accessed=20 * length * width,
            transcendentals=8 * length * width,
        ),
        name="rec_fwd",
    )(proj, lb[None], gain[None])


def rec_bwd(proj, states, dmix, lb):
    length, width = proj.shape[0], lb.shape[0]
    spans, heads = length // SPAN, width // HEAD
    dproj, glb = pl.pallas_call(
        rec_bwd_kernel,
        grid=(spans,),
        in_specs=[
            pl.BlockSpec((SPAN, 3 * width), lambda i: (spans - 1 - i, 0)),
            pl.BlockSpec((1, heads, HEAD, HEAD), lambda i: (spans - 1 - i, 0, 0, 0)),
            pl.BlockSpec((SPAN, width), lambda i: (spans - 1 - i, 0)),
            pl.BlockSpec((1, width), lambda i: (0, 0)),
        ],
        out_specs=[
            pl.BlockSpec((SPAN, 3 * width), lambda i: (spans - 1 - i, 0)),
            pl.BlockSpec((8, width), lambda i: (0, 0)),
        ],
        out_shape=[
            jax.ShapeDtypeStruct((length, 3 * width), jnp.bfloat16),
            jax.ShapeDtypeStruct((8, width), jnp.float32),
        ],
        scratch_shapes=[pltpu.VMEM((heads, HEAD, HEAD), jnp.float32)],
        cost_estimate=pl.CostEstimate(
            flops=20 * length * SPAN * width,
            bytes_accessed=30 * length * width,
            transcendentals=8 * length * width,
        ),
        name="rec_bwd",
    )(proj, states, dmix, lb[None])
    return dproj, glb[0]


def neighbour_barrier(place, count, right, left):
    barrier = pltpu.get_barrier_semaphore()

    @pl.when(place > 0)
    def _():
        pl.semaphore_signal(
            barrier, inc=1, device_id={"seq": left}, device_id_type=pl.DeviceIdType.MESH
        )

    @pl.when(place < count - 1)
    def _():
        pl.semaphore_signal(
            barrier, inc=1, device_id={"seq": right}, device_id_type=pl.DeviceIdType.MESH
        )

    inner = jnp.logical_and(place > 0, place < count - 1)

    @pl.when(inner)
    def _():
        pl.semaphore_wait(barrier, 2)

    @pl.when(jnp.logical_not(inner))
    def _():
        pl.semaphore_wait(barrier, 1)


def send(source, target, send_sem, recv_sem, device):
    return pltpu.make_async_remote_copy(
        src_ref=source,
        dst_ref=target,
        send_sem=send_sem,
        recv_sem=recv_sem,
        device_id={"seq": device},
        device_id_type=pl.DeviceIdType.MESH,
    )


def each(count, step):
    def run(i, carry):
        step(i)
        return carry

    lax.fori_loop(0, count, run, 0)


def relay(place, count, pass_right, pass_left, finish):
    def run(early, late):
        def step(i):
            @pl.when(i < PIECES)
            def _():
                early(i)

            @pl.when(i >= LAG)
            def _():
                late(i - LAG)

        each(PIECES + LAG, step)
        each(PIECES, finish)

    @pl.when(jnp.logical_and(place > 0, place < count // 2))
    def _():
        run(pass_right, pass_left)

    @pl.when(jnp.logical_and(place >= count // 2, place < count - 1))
    def _():
        run(pass_left, pass_right)


def line_gather_kernel(count, x_ref, out_ref, send_right, recv_right, send_left, recv_left, own_sem):
    place = lax.axis_index("seq")
    right, left = lax.rem(place + 1, count), lax.rem(place + count - 1, count)
    half = x_ref.shape[0]
    rows = half // PIECES
    neighbour_barrier(place, count, right, left)

    def low(i):
        return out_ref.at[pl.ds(pl.multiple_of(i * rows, rows), rows)]

    def high(i):
        return out_ref.at[pl.ds(pl.multiple_of(half + i * rows, rows), rows)]

    def own(i):
        return x_ref.at[pl.ds(pl.multiple_of(i * rows, rows), rows)]

    def rightward(i, source):
        return send(source, low(i), send_right.at[i], recv_right.at[i], right)

    def leftward(i, source):
        return send(source, high(i), send_left.at[i], recv_left.at[i], left)

    @pl.when(place == 0)
    def _():
        each(PIECES, lambda i: rightward(i, own(i)).start())
        keep = pltpu.make_async_copy(x_ref, out_ref.at[pl.ds(0, half)], own_sem)
        keep.start()
        each(PIECES, lambda i: leftward(i, high(i)).wait_recv())
        keep.wait()
        each(PIECES, lambda i: rightward(i, own(i)).wait_send())

    @pl.when(place == count - 1)
    def _():
        each(PIECES, lambda i: leftward(i, own(i)).start())
        keep = pltpu.make_async_copy(x_ref, out_ref.at[pl.ds(half, half)], own_sem)
        keep.start()
        each(PIECES, lambda i: rightward(i, low(i)).wait_recv())
        keep.wait()
        each(PIECES, lambda i: leftward(i, own(i)).wait_send())

    def pass_right(i):
        moving = rightward(i, low(i))
        moving.wait_recv()
        moving.start()

    def pass_left(i):
        moving = leftward(i, high(i))
        moving.wait_recv()
        moving.start()

    def finish(i):
        rightward(i, low(i)).wait_send()
        leftward(i, high(i)).wait_send()

    relay(place, count, pass_right, pass_left, finish)


def line_scatter_kernel(
    count, x_ref, out_ref, got_right, got_left, sum_right, sum_left,
    send_right, recv_right, send_left, recv_left,
):
    place = lax.axis_index("seq")
    right, left = lax.rem(place + 1, count), lax.rem(place + count - 1, count)
    half = out_ref.shape[0]
    rows = half // PIECES
    neighbour_barrier(place, count, right, left)

    def cut(i):
        return pl.ds(pl.multiple_of(i * rows, rows), rows)

    def low(i):
        return x_ref.at[cut(i)]

    def high(i):
        return x_ref.at[pl.ds(pl.multiple_of(half + i * rows, rows), rows)]

    def rightward(i, source):
        return send(source, got_right.at[cut(i)], send_right.at[i], recv_right.at[i], right)

    def leftward(i, source):
        return send(source, got_left.at[cut(i)], send_left.at[i], recv_left.at[i], left)

    def added(got, mine):
        return got[...].astype(jnp.float32) + mine[...].astype(jnp.float32)

    @pl.when(place == 0)
    def _():
        each(PIECES, lambda i: rightward(i, high(i)).start())

        def close(i):
            leftward(i, low(i)).wait_recv()
            out_ref[cut(i), :] = added(got_left.at[cut(i)], low(i))

        each(PIECES, close)
        each(PIECES, lambda i: rightward(i, high(i)).wait_send())

    @pl.when(place == count - 1)
    def _():
        each(PIECES, lambda i: leftward(i, low(i)).start())

        def close(i):
            rightward(i, high(i)).wait_recv()
            out_ref[cut(i), :] = added(got_right.at[cut(i)], high(i))

        each(PIECES, close)
        each(PIECES, lambda i: leftward(i, low(i)).wait_send())

    def pass_right(i):
        moving = rightward(i, sum_right.at[cut(i)])
        moving.wait_recv()
        sum_right[cut(i), :] = added(got_right.at[cut(i)], high(i)).astype(sum_right.dtype)
        moving.start()

    def pass_left(i):
        moving = leftward(i, sum_left.at[cut(i)])
        moving.wait_recv()
        sum_left[cut(i), :] = added(got_left.at[cut(i)], low(i)).astype(sum_left.dtype)
        moving.start()

    def finish(i):
        rightward(i, sum_right.at[cut(i)]).wait_send()
        leftward(i, sum_left.at[cut(i)]).wait_send()
        out_ref[cut(i), :] = jnp.zeros((rows, out_ref.shape[1]), out_ref.dtype)

    relay(place, count, pass_right, pass_left, finish)


def gather_rows(array):
    half, width = array.shape
    count = lax.axis_size("seq")
    return pl.pallas_call(
        functools.partial(line_gather_kernel, count),
        in_specs=[pl.BlockSpec(memory_space=pltpu.VMEM)],
        out_specs=pl.BlockSpec(memory_space=pltpu.VMEM),
        out_shape=jax.ShapeDtypeStruct((2 * half, width), array.dtype),
        scratch_shapes=[pltpu.SemaphoreType.DMA((PIECES,))] * 4 + [pltpu.SemaphoreType.DMA],
        compiler_params=pltpu.CompilerParams(collective_id=0, has_side_effects=True),
        cost_estimate=pl.CostEstimate(
            flops=0, bytes_accessed=80 * half * width, transcendentals=0
        ),
        name="line_gather",
    )(array)


def scatter_rows(array):
    rows, width = array.shape
    half = rows // 2
    count = lax.axis_size("seq")
    return pl.pallas_call(
        functools.partial(line_scatter_kernel, count),
        in_specs=[pl.BlockSpec(memory_space=pltpu.VMEM)],
        out_specs=pl.BlockSpec(memory_space=pltpu.VMEM),
        out_shape=jax.ShapeDtypeStruct((half, width), jnp.float32),
        scratch_shapes=[pltpu.VMEM((half, width), array.dtype)] * 4
        + [pltpu.SemaphoreType.DMA((PIECES,))] * 4,
        compiler_params=pltpu.CompilerParams(collective_id=1, has_side_effects=True),
        cost_estimate=pl.CostEstimate(
            flops=0, bytes_accessed=80 * half * width, transcendentals=0
        ),
        name="line_scatter",
    )(array)


def other_core(array):
    return lax.ppermute(array, "pipe", [(0, 1), (1, 0)])


def small_sum(array, axis):
    size = lax.axis_size(axis)
    if size > 4:
        return lax.psum(array, axis)
    total = array
    for step in range(1, size):
        total = total + lax.ppermute(array, axis, [(i, (i + step) % size) for i in range(size)])
    return total


def pick(first, zero, one):
    return jnp.where(first, zero, one)


def inverse_rms(values_in):
    return lax.rsqrt(jnp.mean(values_in * values_in, axis=-1, keepdims=True) + EPSILON)


def norm_backward(values_in, gain, grad):
    inv = inverse_rms(values_in)
    unit = values_in * inv
    grad_gain = jnp.sum(grad * unit, axis=0)
    scaled = grad * gain
    return inv * (scaled - unit * jnp.mean(scaled * unit, axis=-1, keepdims=True)), grad_gain


def dot(left, right, left_dim, right_dim, kind=jnp.float32):
    return lax.dot_general(
        left, right, (((left_dim,), (right_dim,)), ((), ())), preferred_element_type=jnp.float32
    ).astype(kind)


def core_half(grad):
    core = lax.axis_index("pipe")
    rows, columns = grad.shape
    halves = grad.reshape(2, rows // 2, columns)
    keep = lax.dynamic_index_in_dim(halves, core, 0, keepdims=False)
    away = lax.dynamic_index_in_dim(halves, 1 - core, 0, keepdims=False)
    received = other_core(away)
    return (keep.astype(jnp.float32) + received.astype(jnp.float32)).astype(jnp.bfloat16)


def row_sum(halves, previous):
    if previous is not None:
        halves, previous = lax.optimization_barrier((halves, previous))
    return lax.psum(halves, "dp"), previous


def finish_sum(zero, one):
    first = lax.axis_index("pipe") == 0
    own = pick(first, zero, one)
    received = other_core(pick(first, one, zero))
    return jnp.concatenate([pick(first, own, received), pick(first, received, own)]).astype(
        jnp.float32
    )


def body(
    inputs,
    cotangent,
    lengths,
    norm_gain,
    w_query,
    w_forget,
    w_input,
    lower_bound,
    out_gain,
    w_output,
    ffn_gain,
    w_gate,
    w_up,
    w_down,
):
    local_rows, width = inputs.shape[2], inputs.shape[3]
    local_width = w_query.shape[2]
    hidden_here = w_gate.shape[2]
    line = lax.axis_size("seq")
    slots = local_rows * line
    half = slots // 2
    core = lax.axis_index("pipe")
    row = lax.axis_index("dp")
    place = lax.axis_index("seq")
    first = core == 0
    bf16 = jnp.bfloat16
    at_end = jnp.logical_or(place == 0, place == line - 1)
    at_end_weight = at_end.astype(jnp.float32)
    half_start = (place >= line // 2).astype(jnp.int32) * half

    def own_half(array):
        return lax.dynamic_slice_in_dim(array, half_start, half, 0)

    def own_rows(array):
        return lax.dynamic_slice_in_dim(array, place * local_rows, local_rows, 0)

    def from_ends(array):
        if line > 4:
            whole = lax.all_gather(array, "seq", axis=0, tiled=False)
            return own_rows(jnp.concatenate([whole[0], whole[line - 1]]))
        quarters = array.reshape(2, local_rows, width)
        moved = lax.ppermute(
            pick(place == 0, quarters[1], quarters[0]), "seq", [(0, 1), (3, 2)]
        )
        kept = pick(place == 0, quarters[0], quarters[1])
        return pick(at_end, kept, moved)

    def gather_all(array):
        return lax.all_gather(array, "seq", axis=0, tiled=True)

    def both(array):
        return lax.all_gather(array, "pipe", axis=0, tiled=False)

    block_in = gather_all(lax.dynamic_index_in_dim(inputs, core, 0, keepdims=False)[0])
    gains = both(jnp.stack([norm_gain[0], ffn_gain[0]]))
    bounds = both(jnp.stack([lower_bound[0], out_gain[0]]))
    w_proj_both = both(jnp.concatenate([w_query[0], w_forget[0], w_input[0]], axis=1).astype(bf16))
    w_out_both = both(w_output[0].astype(bf16))
    w_pair_both = both(jnp.concatenate([w_gate[0], w_up[0]], axis=1).astype(bf16))
    w_down_both = both(w_down[0].astype(bf16))

    own_length = lax.dynamic_slice(lengths, (core, row), (1, 1))[0, 0]
    mask_all = (jnp.arange(slots, dtype=jnp.int32) < own_length).astype(jnp.float32)[:, None]
    mask = own_half(mask_all)
    source_grad = gather_all(lax.dynamic_index_in_dim(cotangent, core, 0, keepdims=False)[0])

    saved = []
    outs = []
    for section in range(2):
        residual_all = block_in.astype(jnp.float32)
        normed_all = (residual_all * inverse_rms(residual_all) * gains[section, 0]).astype(bf16)
        residual_low = own_half(block_in)
        residual = residual_low.astype(jnp.float32)
        projected = dot(normed_all, w_proj_both[section], 1, 0)
        head_gain = bounds[section, 1]
        mixed_gain, squares, states = rec_fwd(projected, bounds[section, 0], head_gain)
        squares = small_sum(squares[0], "seq")
        branch = scatter_rows(dot(mixed_gain, w_out_both[section], 1, 0, bf16))
        inv_mix = lax.rsqrt(own_half(squares) / width + EPSILON)[:, None]
        branch = branch * inv_mix
        middle = residual + branch
        normed_two = (middle * inverse_rms(middle) * gains[section, 1]).astype(bf16)
        normed_two_all = gather_rows(normed_two)
        paired = dot(normed_two_all, w_pair_both[section], 1, 0, bf16)
        gate_act = paired[:, :hidden_here].astype(jnp.float32)
        up_act = paired[:, hidden_here:].astype(jnp.float32)
        hidden = (jax.nn.silu(gate_act) * up_act).astype(bf16)
        ffn_branch = scatter_rows(dot(hidden, w_down_both[section], 1, 0, bf16))
        out_low = (mask * (middle + ffn_branch)).astype(bf16)
        saved.append(
            (residual_low, normed_all, projected, mixed_gain, states, inv_mix, branch, middle)
            + (normed_two_all, paired, hidden)
        )
        if section == 0:
            block_in = gather_rows(out_low)
            outs.append(own_rows(block_in))
        else:
            outs.append(from_ends(out_low))

    small = [None, None]
    sums = [None, None]
    grad_ins = [None, None]
    summed = None
    grad_branch_all = (mask_all * source_grad.astype(jnp.float32)).astype(bf16)
    masked = own_half(grad_branch_all).astype(jnp.float32)
    for section in (1, 0):
        residual_low, normed_all, projected, mixed_gain, states, inv_mix, branch, middle = saved[
            section
        ][:8]
        residual = residual_low.astype(jnp.float32)
        normed_two_all, paired, hidden = saved[section][8:]
        head_gain = bounds[section, 1]
        grad_hidden = dot(grad_branch_all, w_down_both[section], 1, 1)
        gate_act = paired[:, :hidden_here].astype(jnp.float32)
        up_act = paired[:, hidden_here:].astype(jnp.float32)
        sig = jax.nn.sigmoid(gate_act)
        grad_up = grad_hidden * gate_act * sig
        grad_gate = grad_hidden * up_act * sig * (1.0 + gate_act * (1.0 - sig))
        grad_pair = jnp.concatenate([grad_gate.astype(bf16), grad_up.astype(bf16)], axis=1)
        grad_down = core_half(dot(hidden, grad_branch_all, 0, 0, bf16))
        grad_pair_weight = core_half(dot(normed_two_all, grad_pair, 0, 0, bf16))
        ffn_sums, previous = row_sum((grad_down, grad_pair_weight), summed)
        if previous is not None:
            sums[1] = sums[1][:1] + [previous]
        grad_normed_two = scatter_rows(dot(grad_pair, w_pair_both[section], 1, 1, bf16))
        from_norm, grad_gain_two = norm_backward(middle, gains[section, 1], grad_normed_two)
        grad_middle = masked + from_norm
        inner = jnp.sum(grad_middle * branch, axis=1)
        factor = inv_mix[:, 0] * inv_mix[:, 0] * inner * (at_end_weight / width)
        factor_all = small_sum(
            lax.dynamic_update_slice(jnp.zeros((slots,), jnp.float32), factor, (half_start,)),
            "seq",
        )
        grad_mix_all = gather_rows((grad_middle * inv_mix).astype(bf16))
        grad_head = dot(grad_mix_all, w_out_both[section], 1, 1)
        mixed = mixed_gain.astype(jnp.float32) / head_gain
        grad_head_gain = jnp.sum(grad_head * mixed, axis=0)
        grad_mixed = (grad_head * head_gain - mixed * factor_all[:, None]).astype(bf16)
        grad_proj, grad_bound = rec_bwd(projected, states, grad_mixed, bounds[section, 0])
        grad_out_weight = core_half(dot(mixed_gain, grad_mix_all, 0, 0, bf16))
        grad_proj_weight = core_half(dot(normed_all, grad_proj, 0, 0, bf16))
        mix_sums, ffn_sums = row_sum((grad_out_weight, grad_proj_weight), ffn_sums)
        summed = mix_sums
        sums[section] = [ffn_sums, mix_sums]
        grad_normed = scatter_rows(dot(grad_proj, w_proj_both[section], 1, 1, bf16))
        from_first, grad_gain_one = norm_backward(residual, gains[section, 0], grad_normed)
        grad_in = grad_middle + from_first
        grad_ins[section] = from_ends(grad_in)
        if section == 1:
            masked_low = (mask * grad_in).astype(bf16)
            masked = masked_low.astype(jnp.float32)
            grad_branch_all = gather_rows(masked_low)
        spread = jnp.zeros((2, width), jnp.float32)
        spread = lax.dynamic_update_slice(
            spread, jnp.stack([grad_bound, grad_head_gain]), (0, place * local_width)
        )
        partial = jnp.concatenate(
            [jnp.stack([grad_gain_one, grad_gain_two]) * at_end_weight, spread]
        )
        small[section] = small_sum(small_sum(small_sum(partial, "pipe"), "seq"), "dp")

    small_own = pick(first, small[0], small[1])
    local_small = lax.dynamic_slice(small_own, (2, place * local_width), (2, local_width))
    zeros, ones = [group[0] + group[1] for group in sums]
    grad_down, grad_pair_weight, grad_out_weight, grad_proj_weight = [
        finish_sum(zero, one) for zero, one in zip(zeros, ones)
    ]

    def exchange(zero, one):
        own = pick(first, zero, one)
        received = other_core(pick(first, one, zero))
        return jnp.stack([pick(first, own, received), pick(first, received, own)])[None, :, None]

    return (
        exchange(outs[0], outs[1]),
        exchange(grad_ins[0], grad_ins[1]),
        small_own[0][None],
        grad_proj_weight[:, :local_width][None],
        grad_proj_weight[:, local_width : 2 * local_width][None],
        grad_proj_weight[:, 2 * local_width :][None],
        local_small[0][None],
        local_small[1][None],
        grad_out_weight[None],
        small_own[1][None],
        grad_pair_weight[:, :hidden_here][None],
        grad_pair_weight[:, hidden_here:][None],
        grad_down[None],
    )


def solution(mesh):
    in_specs = (
        P(None, "dp", "seq", None),
        P(None, "dp", "seq", None),
        P(),
        P("pipe", None),
        P("pipe", None, "seq"),
        P("pipe", None, "seq"),
        P("pipe", None, "seq"),
        P("pipe", "seq"),
        P("pipe", "seq"),
        P("pipe", "seq", None),
        P("pipe", None),
        P("pipe", None, "seq"),
        P("pipe", None, "seq"),
        P("pipe", "seq", None),
    )
    out_specs = (
        P("pipe", None, "dp", "seq", None),
        P("pipe", None, "dp", "seq", None),
        P("pipe", None),
        P("pipe", None, "seq"),
        P("pipe", None, "seq"),
        P("pipe", None, "seq"),
        P("pipe", "seq"),
        P("pipe", "seq"),
        P("pipe", "seq", None),
        P("pipe", None),
        P("pipe", None, "seq"),
        P("pipe", None, "seq"),
        P("pipe", "seq", None),
    )
    return jax.shard_map(body, mesh=mesh, in_specs=in_specs, out_specs=out_specs, check_vma=False)
```
